32 devices in a mesh: sub: 2 (over x), strip: 16 (over z, y, core).
Axes of the slice: x: 2, y: 2, z: 4, core: 2. Of those that a mesh axis runs over, the one named last changes fastest.
Arguments:
- forcing: float32 [2, 2048, 2048], P('sub', 'strip'), may hold values from -6 to 6
- mult_start: float32 [2, 2048, 2048], P('sub', 'strip'), may hold values from -6 to 6
- incr_start: float32 [2, 2048, 2048], P('sub', 'strip'), may hold values from -6 to 6
- diffusivity: float32 [2, 2048, 2048], P('sub', 'strip'), may hold values from 0.02 to 0.24
- north_corr: bfloat16 [2048, 2048], P('strip'), may hold values from -0.07629126 to 1.07629126
- east_corr: bfloat16 [2048, 2048], replicated, may hold values from -0.07629126 to 1.07629126
Outputs:
- mult_resid: float32 [2, 2048, 2048], P('sub', 'strip')
- grad_resid: float32 [2, 2048, 2048], P('sub', 'strip')
The draws below stay inside these ranges and needn't reach their ends.
All inputs are finite; a program needn't handle non-finite values.
Results may differ from the reference program's by a relative error of at most 0.014.
Values may be sent and summed in bfloat16 or wider, within the bound.
No kernel may reach another device: no remote copies, remote signals or barrier semaphores. Data moves between devices by JAX's collectives and lax.ppermute only.
A program may use at most 128 MiB of HBM per device.

```python
import math
import jax
import jax.numpy as jnp
from jax import lax

NX = 2048
NY = 2048
STEPS = 4
ITERS = 2
SUBW = 2


def corr_matrix(key, matrix_order):
    entries = jax.random.normal(key, (matrix_order, matrix_order), jnp.float32)
    entries = jnp.clip(entries, -6.0, 6.0)
    return (jnp.eye(matrix_order, dtype=jnp.float32) + 0.5 * entries / math.sqrt(matrix_order)).astype(jnp.bfloat16)


def draw_north_corr(key, part):
    return corr_matrix(jax.random.fold_in(key, 11), NX)


def draw_east_corr(key, part):
    return corr_matrix(jax.random.fold_in(key, 12), NY)


def shard_levels(rng, shape, cuts, least, high):
    level = 1.0
    for position, blocks in cuts:
        steps = jax.random.uniform(jax.random.fold_in(jax.random.fold_in(rng, 6), position), (blocks,), jnp.float32, least / len(cuts), high / len(cuts))
        level = level * jnp.repeat(jnp.exp(steps), shape[position] // blocks).reshape((-1,) + (1,) * (len(shape) - 1 - position))
    return level


def normal_values(own_key, dims, scale, most, cuts=(), held_as=jnp.bfloat16):
    values = scale * jax.random.normal(own_key, dims, jnp.float32)
    if cuts:
        values = values * shard_levels(own_key, dims, cuts, -0.22, 0.18)
    return jnp.clip(values, -most, most).astype(held_as)


def setup_inputs(seed: int = 0) -> dict:
    arg_keys = jax.random.split(jax.random.key(seed), 7)
    return {
        "forcing": normal_values(arg_keys[0], (SUBW, NX, NY), 1.0, 6.0, ((0, 2), (1, 16)), jnp.float32),
        "mult_start": normal_values(arg_keys[1], (SUBW, NX, NY), 1.0, 6.0, ((0, 2), (1, 16)), jnp.float32),
        "incr_start": normal_values(arg_keys[2], (SUBW, NX, NY), 1.0, 6.0, ((0, 2), (1, 16)), jnp.float32),
        "diffusivity": jnp.clip(0.02 + 0.22 * jax.random.uniform(arg_keys[3], (SUBW, NX, NY), jnp.float32) ** shard_levels(arg_keys[3], (SUBW, NX, NY), ((0, 2), (1, 16)), -0.2, 0.2), 0.02, 0.24),
        "north_corr": draw_north_corr(jax.random.fold_in(arg_keys[6], 71), 0),
        "east_corr": draw_east_corr(jax.random.fold_in(arg_keys[6], 71), 0),
    }


step_weight = 0.5


def laplace(field):
    padded = jnp.pad(field, ((0, 0), (1, 1), (1, 1)))
    return (padded[:, :-2, 1:-1] + padded[:, 2:, 1:-1] + padded[:, 1:-1, :-2]
            + padded[:, 1:-1, 2:] - 4.0 * padded[:, 1:-1, 1:-1])


def propagate(field, diffuse):
    for each_step in range(STEPS):
        field = field + diffuse * laplace(field)
    return field


def adjoint(field, diffuse):
    for each_step in range(STEPS):
        field = field + laplace(diffuse * field)
    return field


def forward_op(increment, diffusivity):
    moved = propagate(increment[:-1], diffusivity[:-1])
    return increment - jnp.concatenate([jnp.zeros_like(increment[:1]), moved], axis=0)


def backward_op(multiplier, diffusivity):
    pulled = adjoint(multiplier[1:], diffusivity[:-1])
    return multiplier - jnp.concatenate([pulled, jnp.zeros_like(multiplier[:1])], axis=0)


def correlate(field, north_corr, east_corr):
    north = north_corr.astype(jnp.float32)
    east = east_corr.astype(jnp.float32)

    def single(sheet):
        lowered = lax.optimization_barrier(sheet.astype(jnp.bfloat16)).astype(jnp.float32)
        north_half = jnp.dot(north, lowered, precision=lax.Precision.HIGHEST)
        north_half = lax.optimization_barrier(north_half.astype(jnp.bfloat16)).astype(jnp.float32)
        return jnp.dot(north_half, east, precision=lax.Precision.HIGHEST)

    return lax.map(single, field)


def reference(forcing, mult_start, incr_start, diffusivity, north_corr, east_corr):
    multiplier = mult_start
    increment = incr_start
    for iteration in range(ITERS):
        multiplier = multiplier + step_weight * (forcing - correlate(multiplier, north_corr, east_corr)
                                                 - forward_op(increment, diffusivity))
        increment = increment + step_weight * backward_op(multiplier, diffusivity)
    mult_resid = forcing - correlate(multiplier, north_corr, east_corr) - forward_op(increment, diffusivity)
    grad_resid = backward_op(multiplier, diffusivity)
    return mult_resid, grad_resid
```

```python
import jax
import jax.numpy as jnp
from jax import lax
from jax.sharding import PartitionSpec as P

STEPS = 4
ITERS = 2

step_weight = 0.5
BOTH = ("sub", "strip")


def split_strip(size):
    core = 2 if size % 2 == 0 else 1
    chips = size // core
    outer = 4 if chips % 4 == 0 else 1
    return outer, chips // outer, core


def laplace(padded):
    widened = jnp.pad(padded, ((0, 0), (1, 1)))
    return (
        widened[:-2, 1:-1]
        + widened[2:, 1:-1]
        + widened[1:-1, :-2]
        + widened[1:-1, 2:]
        - 4.0 * widened[1:-1, 1:-1]
    )


def local(forcing, mult_start, incr_start, diffusivity, north_corr, east_corr):
    forcing = forcing[0]
    diffuse = diffusivity[0]
    rows, cols = forcing.shape
    strips = lax.axis_size("strip")
    subs = lax.axis_size("sub")
    nz, ny, nk = split_strip(strips)
    width = cols // nz
    strip = lax.axis_index("strip")
    sub = lax.axis_index("sub")
    my_z, my_y, my_k = strip // (ny * nk), (strip // nk) % ny, strip % nk

    def send(value, move):
        pairs = []
        for s in range(subs):
            for t in range(strips):
                to = move(s, t)
                if to is not None:
                    pairs.append((s * strips + t, to[0] * strips + to[1]))
        return lax.ppermute(value, BOTH, pairs)

    def by_z(value, j):
        return send(value, lambda s, t: (s, t ^ (j * ny * nk)))

    def by_y(value, j):
        return send(value, lambda s, t: (s, t ^ (j * nk)))

    def by_k(value, j):
        return send(value, lambda s, t: (s, t ^ j))

    def to_strip(value, step):
        return send(value, lambda s, t: (s, t + step) if 0 <= t + step < strips else None)

    def to_sub(value, step):
        return send(value, lambda s, t: (s + step, t) if 0 <= s + step < subs else None)

    def xor_order(value, axis, index):
        size = value.shape[axis]
        bit = 1
        while bit < size:
            order = [i ^ bit for i in range(size)]
            flipped = jnp.concatenate(
                [lax.slice_in_dim(value, i, i + 1, axis=axis) for i in order], axis=axis
            )
            value = jnp.where((index // bit) % 2 == 1, flipped, value)
            bit *= 2
        return value

    mine = north_corr.reshape(rows, nz, ny, nk, rows)
    mine = xor_order(xor_order(xor_order(mine, 1, my_z), 2, my_y), 3, my_k)
    mine = mine.transpose(0, 3, 2, 1, 4)

    def for_peer(block, j):
        order = [i ^ j for i in range(nz)]
        return jnp.stack([block[:, :, :, i] for i in order], axis=3).reshape(
            block.shape[0], strips * rows
        )

    share = subs % 2 == 0
    north_blocks = [for_peer(mine, 0)]
    if share:
        odd = sub % 2 == 1
        half = jnp.where(odd, mine[rows // 2 :], mine[: rows // 2])
        for j in range(1, nz):
            got = by_z(for_peer(half, j), j)
            other = send(got, lambda s, t: (s ^ 1, t))
            north_blocks.append(
                jnp.where(
                    odd,
                    jnp.concatenate([other, got], axis=0),
                    jnp.concatenate([got, other], axis=0),
                )
            )
    else:
        for j in range(1, nz):
            north_blocks.append(by_z(for_peer(mine, j), j))
    north_rel = jnp.concatenate(north_blocks, axis=0)

    def correlate(field):
        low = field.astype(jnp.bfloat16)
        by_z_own = [
            lax.dynamic_slice_in_dim(low, (my_z ^ j) * width, width, axis=1) for j in range(nz)
        ]
        pieces = [by_z_own[0]] + [by_z(by_z_own[j], j) for j in range(1, nz)]
        tall = [jnp.concatenate(pieces, axis=0)]
        for j in range(1, ny):
            tall.append(jnp.concatenate([by_y(p, j) for p in pieces], axis=0))
        tall = jnp.concatenate(tall, axis=0)
        tall = jnp.concatenate([tall] + [by_k(tall, j) for j in range(1, nk)], axis=0)
        tile = jnp.dot(north_rel, tall, preferred_element_type=jnp.float32).astype(jnp.bfloat16)
        tile = tile.reshape(nz, rows, width)
        back = jnp.stack([tile[0]] + [by_z(tile[j], j) for j in range(1, nz)])
        back = xor_order(back, 0, my_z)
        north_half = back.transpose(1, 0, 2).reshape(rows, cols)
        return jnp.dot(north_half, east_corr, preferred_element_type=jnp.float32)

    deep = 2 * STEPS
    global_rows = strip * rows - deep + lax.iota(jnp.int32, rows + 2 * deep)
    inside = ((global_rows >= 0) & (global_rows < rows * strips)).astype(jnp.float32)[:, None]

    def rims(value, depth):
        before = to_strip(value[rows - depth :], 1)
        after = to_strip(value[:depth], -1)
        return before, after

    short_diffuse = diffuse.astype(jnp.bfloat16)
    short_incr = incr_start[0].astype(jnp.bfloat16)
    packed = jnp.concatenate(
        [short_diffuse[:deep], short_incr[:STEPS], short_diffuse[rows - deep :], short_incr[rows - STEPS :]],
        axis=0,
    )
    size = deep + STEPS
    before = to_strip(packed[size:], 1)
    after = to_strip(packed[:size], -1)
    diffuse_wide = jnp.concatenate(
        [before[:deep].astype(jnp.float32), diffuse, after[:deep].astype(jnp.float32)], axis=0
    )
    incr_wide = jnp.concatenate(
        [before[deep:].astype(jnp.float32), incr_start[0], after[deep:].astype(jnp.float32)],
        axis=0,
    )

    def propagate(widened):
        for each_step in range(STEPS):
            length = widened.shape[0] - 2
            at = STEPS + each_step + 1
            widened = (
                widened[1:-1] + diffuse_wide[at : at + length] * laplace(widened)
            ) * inside[at : at + length]
        return widened

    def adjoint(widened):
        for each_step in range(STEPS):
            length = widened.shape[0] - 2
            weighted = diffuse_wide[each_step : each_step + widened.shape[0]] * widened
            at = each_step + 1
            widened = (widened[1:-1] + laplace(weighted)) * inside[at : at + length]
        return widened

    def forward_op(incr_wide):
        arrived = to_sub(propagate(incr_wide).astype(jnp.bfloat16), 1)
        return incr_wide[STEPS:-STEPS] - arrived

    def gradient(multiplier):
        short = multiplier.astype(jnp.bfloat16)
        above, below = rims(short, deep)
        far = to_sub(short, -1)
        far_rims = to_sub(jnp.concatenate([above, below], axis=0), -1)
        following = jnp.concatenate([far_rims[:deep], far, far_rims[deep:]], axis=0)
        pulled = adjoint(following.astype(jnp.float32))
        here = jnp.concatenate(
            [
                above[deep - STEPS :].astype(jnp.float32),
                multiplier,
                below[:STEPS].astype(jnp.float32),
            ],
            axis=0,
        )
        return here - pulled

    multiplier = mult_start[0]
    for iteration in range(ITERS):
        multiplier = multiplier + step_weight * (
            forcing - correlate(multiplier) - forward_op(incr_wide)
        )
        grad = gradient(multiplier)
        incr_wide = incr_wide + step_weight * grad
    mult_resid = forcing - correlate(multiplier) - forward_op(incr_wide)
    grad_resid = grad[STEPS:-STEPS]
    return (mult_resid[None], grad_resid[None])


def solution(mesh):
    return jax.shard_map(
        local,
        mesh=mesh,
        in_specs=(
            P("sub", "strip", None),
            P("sub", "strip", None),
            P("sub", "strip", None),
            P("sub", "strip", None),
            P("strip", None),
            P(),
        ),
        out_specs=(P("sub", "strip", None), P("sub", "strip", None)),
        check_vma=False,
    )
```

```python
import jax
import jax.numpy as jnp
from jax import lax
from jax.experimental import pallas as pl
from jax.experimental.pallas import tpu as pltpu
from jax.sharding import PartitionSpec as P

STEPS = 4
ITERS = 2

step_weight = 0.5
BOTH = ("sub", "strip")


def split_strip(size):
    core = 2 if size % 2 == 0 else 1
    chips = size // core
    outer = 4 if chips % 4 == 0 else 1
    return outer, chips // outer, core


def laplace(padded):
    widened = jnp.pad(padded, ((0, 0), (1, 1)))
    return (
        widened[:-2, 1:-1]
        + widened[2:, 1:-1]
        + widened[1:-1, :-2]
        + widened[1:-1, 2:]
        - 4.0 * widened[1:-1, 1:-1]
    )


def local(forcing, mult_start, incr_start, diffusivity, north_corr, east_corr):
    forcing = forcing[0]
    diffuse = diffusivity[0]
    rows, cols = forcing.shape
    strips = lax.axis_size("strip")
    subs = lax.axis_size("sub")
    nz, ny, nk = split_strip(strips)
    width = cols // nz
    strip = lax.axis_index("strip")
    sub = lax.axis_index("sub")
    my_z, my_y, my_k = strip // (ny * nk), (strip // nk) % ny, strip % nk

    def send(value, move):
        pairs = []
        for s in range(subs):
            for t in range(strips):
                to = move(s, t)
                if to is not None:
                    pairs.append((s * strips + t, to[0] * strips + to[1]))
        return lax.ppermute(value, BOTH, pairs)

    def by_z(value, j):
        return send(value, lambda s, t: (s, t ^ (j * ny * nk)))

    def by_y(value, j):
        return send(value, lambda s, t: (s, t ^ (j * nk)))

    def by_k(value, j):
        return send(value, lambda s, t: (s, t ^ j))

    def to_strip(value, step):
        return send(value, lambda s, t: (s, t + step) if 0 <= t + step < strips else None)

    def to_sub(value, step):
        return send(value, lambda s, t: (s + step, t) if 0 <= s + step < subs else None)

    half = rows // 2
    north_blocks = {0: (north_corr[:half], north_corr[half:])}
    bit = nz // 2
    while bit >= 1:
        for j, parts in list(north_blocks.items()):
            north_blocks[j ^ bit] = tuple(by_z(part, bit) for part in parts)
        bit //= 2
    north_rel = jnp.concatenate([part for j in range(nz) for part in north_blocks[j]], axis=0)

    place = jnp.stack([my_z, my_y, my_k]).astype(jnp.int32)
    scalars = pl.BlockSpec(memory_space=pltpu.SMEM)
    whole = pl.BlockSpec(memory_space=pltpu.VMEM)
    hops = [(jk, jy, jz) for jk in range(nk) for jy in range(ny) for jz in range(nz)]

    def cut(low):
        return [lax.dynamic_slice_in_dim(low, (my_z ^ j) * width, width, axis=1) for j in range(nz)]

    def spread(own):
        held = {(0, 0, j): own[j] if j == 0 else by_z(own[j], j) for j in range(nz)}
        for jk, jy, jz in hops:
            if jk == 0 and jy > 0:
                held[0, jy, jz] = by_y(held[0, 0, jz], jy)
        for jk, jy, jz in hops:
            if jk > 0:
                held[jk, jy, jz] = by_k(held[0, jy, jz], jk)
        return [held[hop] for hop in hops]

    def north_body(at, north, *refs):
        pieces, outs, tall = refs[: len(hops)], refs[len(hops) : -1], refs[-1]
        for (jk, jy, jz), piece in zip(hops, pieces):
            strip_at = ((at[0] ^ jz) * ny + (at[1] ^ jy)) * nk + (at[2] ^ jk)
            tall[pl.ds(pl.multiple_of(strip_at * rows, rows), rows), :] = piece[...]
        tile = jnp.dot(north[...], tall[...], preferred_element_type=jnp.float32)
        for j in range(nz):
            outs[j][...] = tile[j * rows : (j + 1) * rows].astype(jnp.bfloat16)

    def product(pieces):
        return pl.pallas_call(
            north_body,
            out_shape=[jax.ShapeDtypeStruct((rows, width), jnp.bfloat16)] * nz,
            in_specs=[scalars] + [whole] * (1 + len(hops)),
            out_specs=[whole] * nz,
            scratch_shapes=[pltpu.VMEM((strips * rows, width), jnp.bfloat16)],
            name="north",
        )(place, north_rel, *pieces)

    def assembled(at, parts, east, half_done):
        for j in range(nz):
            col = pl.multiple_of((at[0] ^ j) * width, width)
            half_done[:, pl.ds(col, width)] = parts[j][...]
        return jnp.dot(half_done[...], east[...], preferred_element_type=jnp.float32)

    def step_body(at, east, target, mult, *refs):
        parts, new, low, cuts, half_done = refs[:nz], refs[nz], refs[nz + 1], refs[nz + 2 : -1], refs[-1]
        value = mult[...] + step_weight * (target[...] - assembled(at, parts, east, half_done))
        new[...] = value
        low[...] = value.astype(jnp.bfloat16)
        for j in range(nz):
            col = pl.multiple_of((at[0] ^ j) * width, width)
            cuts[j][...] = low[:, pl.ds(col, width)]

    def last_body(at, east, target, *refs):
        parts, out, half_done = refs[:nz], refs[nz], refs[-1]
        out[...] = target[...] - assembled(at, parts, east, half_done)

    def finish(body, outs, tile, *fields):
        parts = [tile[0]] + [by_z(tile[j], j) for j in range(1, nz)]
        return pl.pallas_call(
            body,
            out_shape=outs,
            in_specs=[scalars] + [whole] * (1 + len(fields) + nz),
            out_specs=[whole] * len(outs),
            scratch_shapes=[pltpu.VMEM((rows, cols), jnp.bfloat16)],
            name="east",
        )(place, east_corr, *fields, *parts)

    field_f32 = jax.ShapeDtypeStruct((rows, cols), jnp.float32)
    field_bf16 = jax.ShapeDtypeStruct((rows, cols), jnp.bfloat16)
    cut_bf16 = jax.ShapeDtypeStruct((rows, width), jnp.bfloat16)

    deep = 2 * STEPS
    global_rows = strip * rows - deep + lax.iota(jnp.int32, rows + 2 * deep)
    inside = ((global_rows >= 0) & (global_rows < rows * strips)).astype(jnp.float32)[:, None]

    short = jnp.concatenate(
        [diffuse.astype(jnp.bfloat16), incr_start[0].astype(jnp.bfloat16)], axis=0
    )
    size = deep + STEPS
    packed = jnp.concatenate(
        [short[:deep], short[rows : rows + STEPS], short[rows - deep : rows], short[2 * rows - STEPS :]],
        axis=0,
    )
    before = to_strip(packed[size:], 1)
    after = to_strip(packed[:size], -1)
    far = to_sub(short, 1).astype(jnp.float32)
    far_rims = to_sub(jnp.concatenate([before, after], axis=0), 1).astype(jnp.float32)
    diffuse_wide = jnp.concatenate(
        [far_rims[:deep], far[:rows], far_rims[size : size + deep]], axis=0
    )
    past_wide = jnp.concatenate(
        [far_rims[deep:size], far[rows:], far_rims[size + deep :]], axis=0
    )
    has_past = (sub > 0).astype(jnp.float32)

    def propagate(widened):
        for each_step in range(STEPS):
            length = widened.shape[0] - 2
            at = STEPS + each_step + 1
            widened = (
                widened[1:-1] + diffuse_wide[at : at + length] * laplace(widened)
            ) * inside[at : at + length]
        return widened

    def adjoint(widened):
        for each_step in range(STEPS):
            length = widened.shape[0] - 2
            weighted = diffuse_wide[each_step : each_step + widened.shape[0]] * widened
            at = each_step + 1
            widened = (widened[1:-1] + laplace(weighted)) * inside[at : at + length]
        return widened

    def launch(multiplier, low):
        above = to_strip(low[rows - deep :], 1)
        below = to_strip(low[:deep], -1)
        pulled = adjoint(
            jnp.concatenate(
                [above.astype(jnp.float32), multiplier, below.astype(jnp.float32)], axis=0
            )
        )
        following = to_sub(pulled[STEPS:-STEPS].astype(jnp.bfloat16), -1)
        past = to_sub(low, 1)
        past_rims = to_sub(
            jnp.concatenate([above[deep - STEPS :], below[:STEPS]], axis=0), 1
        )
        return pulled, following, past, past_rims

    multiplier = mult_start[0]
    incr = incr_start[0]
    tile = product(spread(cut(multiplier.astype(jnp.bfloat16))))
    target = forcing - incr + propagate(past_wide)
    for iteration in range(ITERS):
        multiplier, low, *own = finish(
            step_body, [field_f32, field_bf16] + [cut_bf16] * nz, tile, target, multiplier
        )
        pulled, following, past, past_rims = launch(multiplier, low)
        tile = product(spread(own))
        grad = multiplier - following.astype(jnp.float32)
        incr = incr + step_weight * grad
        past = jnp.concatenate(
            [past_rims[:STEPS], past, past_rims[STEPS:]], axis=0
        ).astype(jnp.float32)
        past_wide = past_wide + step_weight * (past - has_past * pulled)
        target = forcing - incr + propagate(past_wide)
    (mult_resid,) = finish(last_body, [field_f32], tile, target)
    return (mult_resid[None], grad[None])


def solution(mesh):
    return jax.shard_map(
        local,
        mesh=mesh,
        in_specs=(
            P("sub", "strip", None),
            P("sub", "strip", None),
            P("sub", "strip", None),
            P("sub", "strip", None),
            P("strip", None),
            P(),
        ),
        out_specs=(P("sub", "strip", None), P("sub", "strip", None)),
        check_vma=False,
    )
```

```python
import jax
import jax.numpy as jnp
from jax import lax
from jax.experimental import pallas as pl
from jax.experimental.pallas import tpu as pltpu
from jax.sharding import PartitionSpec as P


STEPS = 4
ITERS = 2

step_weight = 0.5
BOTH = ("sub", "strip")


def split_strip(size):
    core = 2 if size % 2 == 0 else 1
    chips = size // core
    outer = 4 if chips % 4 == 0 else 1
    return outer, chips // outer, core


def whole_step(forcing, mult_start, incr_start, diffusivity, north_corr, east_corr):
    forcing = forcing[0]
    diffuse = diffusivity[0]
    rows, cols = forcing.shape
    strips = lax.axis_size("strip")
    subs = lax.axis_size("sub")
    nz, ny, nk = split_strip(strips)
    width = cols // nz
    strip = lax.axis_index("strip")
    sub = lax.axis_index("sub")
    my_z, my_y, my_k = strip // (ny * nk), (strip // nk) % ny, strip % nk

    def send(value, move):
        pairs = []
        for s in range(subs):
            for t in range(strips):
                to = move(s, t)
                if to is not None:
                    pairs.append((s * strips + t, to[0] * strips + to[1]))
        return lax.ppermute(value, BOTH, pairs)

    def by_z(value, j):
        return send(value, lambda s, t: (s, t ^ (j * ny * nk)))

    def by_y(value, j):
        return send(value, lambda s, t: (s, t ^ (j * nk)))

    def by_k(value, j):
        return send(value, lambda s, t: (s, t ^ j))

    def to_strip(value, step):
        return send(value, lambda s, t: (s, t + step) if 0 <= t + step < strips else None)

    def to_sub(value, step):
        return send(value, lambda s, t: (s + step, t) if 0 <= s + step < subs else None)

    def xor_order(value, axis, index):
        size = value.shape[axis]
        bit = 1
        while bit < size:
            order = [i ^ bit for i in range(size)]
            flipped = jnp.concatenate(
                [lax.slice_in_dim(value, i, i + 1, axis=axis) for i in order], axis=axis
            )
            value = jnp.where((index // bit) % 2 == 1, flipped, value)
            bit *= 2
        return value

    half = rows // 2
    north_blocks = {0: (north_corr[:half], north_corr[half:])}
    bit = nz // 2
    while bit >= 1:
        for j, parts in list(north_blocks.items()):
            north_blocks[j ^ bit] = tuple(by_z(part, bit) for part in parts)
        bit //= 2
    north_rel = jnp.concatenate([part for j in range(nz) for part in north_blocks[j]], axis=0)

    def cut(low):
        return [lax.dynamic_slice_in_dim(low, (my_z ^ j) * width, width, axis=1) for j in range(nz)]

    def spread(own):
        side = 2 if nz % 2 == 0 else 1
        held = {0: own[0]}
        for j in [*range(side, nz), *range(1, side)]:
            held[j] = by_z(own[j], j)
        groups = {
            (0, 0, at // side): xor_order(
                jnp.stack([held[j] for j in range(at, at + side)]), 0, my_z % side
            )
            for at in range(0, nz, side)
        }
        for jy in range(1, ny):
            for i in range(nz // side):
                groups[0, jy, i] = by_y(groups[0, 0, i], jy)
        for jk in range(1, nk):
            for jy in range(ny):
                for i in range(nz // side):
                    groups[jk, jy, i] = by_k(groups[0, jy, i], jk)
        tall = jnp.zeros((nz, ny * nk, rows, width), jnp.bfloat16)
        for (jk, jy, i), group in groups.items():
            at = ((my_z // side) ^ i) * side, (my_y ^ jy) * nk + (my_k ^ jk), 0, 0
            tall = lax.dynamic_update_slice(tall, group[:, None], at)
        return tall.reshape(strips * rows, width)

    def product(tall):
        tile = jnp.dot(north_rel, tall, preferred_element_type=jnp.float32).astype(jnp.bfloat16)
        return [tile[j * rows : (j + 1) * rows] for j in range(nz)]

    def finish(tile):
        parts = [tile[0]] + [by_z(tile[j], j) for j in range(1, nz)]
        line = xor_order(jnp.stack(parts), 0, my_z).transpose(1, 0, 2).reshape(rows, cols)
        return jnp.dot(line, east_corr, preferred_element_type=jnp.float32)

    deep = 8
    tall_rows = rows + 2 * deep
    blocks = tall_rows // deep
    whole = pl.BlockSpec(memory_space=pltpu.VMEM)
    scalars = pl.BlockSpec(memory_space=pltpu.SMEM)
    limits = pltpu.CompilerParams(vmem_limit_bytes=20 * 1024 * 1024)
    f32, bf16 = jnp.float32, jnp.bfloat16
    wide_f32 = jax.ShapeDtypeStruct((tall_rows, cols), f32)
    field_f32 = jax.ShapeDtypeStruct((rows, cols), f32)
    field_bf16 = jax.ShapeDtypeStruct((rows, cols), bf16)
    ends = jnp.stack([strip > 0, strip < strips - 1, sub > 0]).astype(f32)

    def rows_at(block):
        return pl.ds(pl.multiple_of(block * deep, deep), deep)

    def laplace(source, block):
        here = source[rows_at(block + 1), :]
        row = lax.broadcasted_iota(jnp.int32, here.shape, 0)
        col = lax.broadcasted_iota(jnp.int32, here.shape, 1)
        above = pltpu.roll(jnp.where(row == deep - 1, source[rows_at(block), :], here), 1, 0)
        below = pltpu.roll(jnp.where(row == 0, source[rows_at(block + 2), :], here), deep - 1, 0)
        left = jnp.where(col == 0, 0.0, pltpu.roll(here, 1, 1))
        right = jnp.where(col == cols - 1, 0.0, pltpu.roll(here, cols - 1, 1))
        return above + below + left + right - 4.0 * here

    def kept(ends_ref, block):
        return jnp.where(block == 0, ends_ref[0], jnp.where(block == blocks - 1, ends_ref[1], 1.0))

    def clear_rims(buffer):
        zero = jnp.zeros((deep, cols), f32)
        for i in range(2):
            buffer[i, :deep, :] = zero
            buffer[i, tall_rows + deep :, :] = zero

    def adjoint_body(ends_ref, mult, above, below, coef, pulled, middle, buffer):
        clear_rims(buffer)
        pulled[:deep, :] = above[...].astype(f32)
        pulled[deep : rows + deep, :] = mult[...]
        pulled[rows + deep :, :] = below[...].astype(f32)

        def weigh(block, carry):
            at = rows_at(block)
            buffer[0, rows_at(block + 1), :] = coef[at, :] * pulled[at, :]
            return carry

        lax.fori_loop(0, blocks, weigh, 0)
        for step in range(STEPS):
            source, target = buffer.at[step % 2], buffer.at[(step + 1) % 2]

            def advance(block, carry):
                at = rows_at(block)
                value = (pulled[at, :] + laplace(source, block)) * kept(ends_ref, block)
                pulled[at, :] = value
                target[rows_at(block + 1), :] = coef[at, :] * value
                return carry

            lax.fori_loop(0, blocks, advance, 0)
        middle[...] = pulled[deep : rows + deep, :].astype(bf16)

    def adjoint(multiplier, above, below):
        return pl.pallas_call(
            adjoint_body,
            out_shape=[wide_f32, field_bf16],
            in_specs=[scalars] + [whole] * 4,
            out_specs=[whole] * 2,
            scratch_shapes=[pltpu.VMEM((2, tall_rows + 2 * deep, cols), f32)],
            compiler_params=limits,
            name="adjoint",
        )(ends, multiplier, above, below, diffuse_wide)

    def propagate(ends_ref, coef, buffer):
        for step in range(STEPS):
            source, target = buffer.at[step % 2], buffer.at[(step + 1) % 2]

            def advance(block, carry):
                at = rows_at(block)
                mid = rows_at(block + 1)
                target[mid, :] = (
                    source[mid, :] + coef[at, :] * laplace(source, block)
                ) * kept(ends_ref, block)
                return carry

            lax.fori_loop(0, blocks, advance, 0)
        return buffer[STEPS % 2, 2 * deep : rows + 2 * deep, :]

    def begin_body(ends_ref, coef, past, forcing_ref, incr, target, buffer):
        clear_rims(buffer)
        buffer[0, deep : tall_rows + deep, :] = past[...]
        target[...] = forcing_ref[...] - incr[...] + propagate(ends_ref, coef, buffer)

    def begin(past, incr):
        return pl.pallas_call(
            begin_body,
            out_shape=field_f32,
            in_specs=[scalars] + [whole] * 4,
            out_specs=whole,
            scratch_shapes=[pltpu.VMEM((2, tall_rows + 2 * deep, cols), f32)],
            compiler_params=limits,
            name="begin",
        )(ends, diffuse_wide, past, forcing, incr)

    def update_body(
        ends_ref, coef, past, arrived, pulled, mult, following, incr, forcing_ref,
        past_new, incr_new, target, grad, buffer
    ):
        clear_rims(buffer)
        past_new[...] = past[...] + step_weight * (
            arrived[...].astype(f32) - ends_ref[2] * pulled[...]
        )
        buffer[0, deep : tall_rows + deep, :] = past_new[...]
        slope = mult[...] - following[...].astype(f32)
        grad[...] = slope
        incr_new[...] = incr[...] + step_weight * slope
        target[...] = forcing_ref[...] - incr_new[...] + propagate(ends_ref, coef, buffer)

    def update(past, arrived, pulled, mult, following, incr):
        return pl.pallas_call(
            update_body,
            out_shape=[wide_f32, field_f32, field_f32, field_f32],
            in_specs=[scalars] + [whole] * 8,
            out_specs=[whole] * 4,
            scratch_shapes=[pltpu.VMEM((2, tall_rows + 2 * deep, cols), f32)],
            compiler_params=limits,
            name="update",
        )(ends, diffuse_wide, past, arrived, pulled, mult, following, incr, forcing)

    short = jnp.concatenate(
        [diffuse.astype(jnp.bfloat16), incr_start[0].astype(jnp.bfloat16)], axis=0
    )
    lowest = jnp.concatenate([short[rows - deep : rows], short[2 * rows - deep :]], axis=0)
    topmost = jnp.concatenate([short[:deep], short[rows : rows + deep]], axis=0)
    before = to_strip(lowest, 1)
    after = to_strip(topmost, -1)
    far = to_sub(short, 1).astype(f32)
    far_rims = to_sub(jnp.concatenate([before, after], axis=0), 1).astype(f32)
    diffuse_wide = jnp.concatenate(
        [far_rims[:deep], far[:rows], far_rims[2 * deep : 3 * deep]], axis=0
    )
    past_wide = jnp.concatenate(
        [far_rims[deep : 2 * deep], far[rows:], far_rims[3 * deep :]], axis=0
    )

    def advance(target, multiplier, incr, past_wide, tile):
        multiplier = multiplier + step_weight * (target - finish(tile))
        low = multiplier.astype(bf16)
        pieces = cut(low)
        above = to_strip(low[rows - deep :], 1)
        below = to_strip(low[:deep], -1)
        pulled, middle = adjoint(multiplier, above, below)
        following = to_sub(middle, -1)
        arrived = to_sub(jnp.concatenate([above, low, below], axis=0), 1)
        tile = product(spread(pieces))
        past_wide, incr, target, grad = update(
            past_wide, arrived, pulled, multiplier, following, incr
        )
        return target, multiplier, incr, past_wide, tile, grad

    multiplier = mult_start[0]
    incr = incr_start[0]
    tile = product(spread(cut(multiplier.astype(jnp.bfloat16))))
    target = begin(past_wide, incr)
    for _ in range(ITERS):
        target, multiplier, incr, past_wide, tile, grad = advance(
            target, multiplier, incr, past_wide, tile
        )
    mult_resid = target - finish(tile)
    return (mult_resid[None], grad[None])


def solution(mesh):
    return jax.shard_map(
        whole_step,
        mesh=mesh,
        in_specs=(
            P("sub", "strip", None),
            P("sub", "strip", None),
            P("sub", "strip", None),
            P("sub", "strip", None),
            P("strip", None),
            P(),
        ),
        out_specs=(P("sub", "strip", None), P("sub", "strip", None)),
        check_vma=False,
    )
```

```python
import jax
import jax.numpy as jnp
from jax import lax
from jax.experimental import pallas as pl
from jax.experimental.pallas import tpu as pltpu
from jax.sharding import PartitionSpec as P


STEPS = 4
ITERS = 2

step_weight = 0.5
BOTH = ("sub", "strip")


def split_strip(size):
    core = 2 if size % 2 == 0 else 1
    chips = size // core
    outer = 4 if chips % 4 == 0 else 1
    return outer, chips // outer, core


def whole_step(forcing, mult_start, incr_start, diffusivity, north_corr, east_corr):
    forcing = forcing[0]
    diffuse = diffusivity[0]
    rows, cols = forcing.shape
    strips = lax.axis_size("strip")
    subs = lax.axis_size("sub")
    nz, ny, nk = split_strip(strips)
    width = cols // nz
    strip = lax.axis_index("strip")
    sub = lax.axis_index("sub")
    my_z, my_y, my_k = strip // (ny * nk), (strip // nk) % ny, strip % nk

    def send(value, move):
        pairs = []
        for s in range(subs):
            for t in range(strips):
                to = move(s, t)
                if to is not None:
                    pairs.append((s * strips + t, to[0] * strips + to[1]))
        return lax.ppermute(value, BOTH, pairs)

    def by_z(value, j):
        return send(value, lambda s, t: (s, t ^ (j * ny * nk)))

    def by_y(value, j):
        return send(value, lambda s, t: (s, t ^ (j * nk)))

    def by_k(value, j):
        return send(value, lambda s, t: (s, t ^ j))

    def to_strip(value, step):
        return send(value, lambda s, t: (s, t + step) if 0 <= t + step < strips else None)

    def to_sub(value, step):
        return send(value, lambda s, t: (s + step, t) if 0 <= s + step < subs else None)

    def xor_order(value, axis, index):
        size = value.shape[axis]
        bit = 1
        while bit < size:
            order = [i ^ bit for i in range(size)]
            flipped = jnp.concatenate(
                [lax.slice_in_dim(value, i, i + 1, axis=axis) for i in order], axis=axis
            )
            value = jnp.where((index // bit) % 2 == 1, flipped, value)
            bit *= 2
        return value

    share = 2 if subs % 2 == 0 and rows % 32 == 0 else 1
    half = rows // share
    first = (sub % share) * half
    gathered = {0: lax.dynamic_slice_in_dim(north_corr, first, half, axis=0)}
    bit = nz // 2
    while bit >= 1:
        for j, part in list(gathered.items()):
            gathered[j ^ bit] = by_z(part, bit)
        bit //= 2
    north_rel = lax.dynamic_update_slice(
        jnp.zeros((nz * rows, strips * rows), jnp.bfloat16), north_corr, (0, 0)
    )
    for j in range(1, nz):
        north_rel = lax.dynamic_update_slice(north_rel, gathered[j], (j * rows + first, 0))
        if share == 2:
            other = send(gathered[j], lambda s, t: (s ^ 1, t))
            north_rel = lax.dynamic_update_slice(north_rel, other, (j * rows + half - first, 0))

    def cut(low):
        return [lax.dynamic_slice_in_dim(low, (my_z ^ j) * width, width, axis=1) for j in range(nz)]

    def spread(own):
        side = 2 if nz % 2 == 0 else 1
        held = {0: own[0]}
        for j in [*range(side, nz), *range(1, side)]:
            held[j] = by_z(own[j], j)
        groups = {
            (0, 0, at // side): xor_order(
                jnp.stack([held[j] for j in range(at, at + side)]), 0, my_z % side
            )
            for at in range(0, nz, side)
        }
        for jy in range(1, ny):
            for i in range(nz // side):
                groups[0, jy, i] = by_y(groups[0, 0, i], jy)
        for jk in range(1, nk):
            for jy in range(ny):
                for i in range(nz // side):
                    groups[jk, jy, i] = by_k(groups[0, jy, i], jk)
        tall = jnp.zeros((nz, ny * nk, rows, width), jnp.bfloat16)
        for (jk, jy, i), group in groups.items():
            at = ((my_z // side) ^ i) * side, (my_y ^ jy) * nk + (my_k ^ jk), 0, 0
            tall = lax.dynamic_update_slice(tall, group[:, None], at)
        return tall.reshape(strips * rows, width)

    def product(tall):
        tile = jnp.dot(north_rel, tall, preferred_element_type=jnp.float32).astype(jnp.bfloat16)
        return [tile[j * rows : (j + 1) * rows] for j in range(nz)]

    def finish(tile):
        parts = [tile[0]] + [by_z(tile[j], j) for j in range(1, nz)]
        line = xor_order(jnp.stack(parts), 0, my_z).transpose(1, 0, 2).reshape(rows, cols)
        return jnp.dot(line, east_corr, preferred_element_type=jnp.float32)

    deep = 8
    tall_rows = rows + 2 * deep
    blocks = tall_rows // deep
    whole = pl.BlockSpec(memory_space=pltpu.VMEM)
    scalars = pl.BlockSpec(memory_space=pltpu.SMEM)
    limits = pltpu.CompilerParams(vmem_limit_bytes=20 * 1024 * 1024)
    f32, bf16 = jnp.float32, jnp.bfloat16
    wide_f32 = jax.ShapeDtypeStruct((tall_rows, cols), f32)
    field_f32 = jax.ShapeDtypeStruct((rows, cols), f32)
    field_bf16 = jax.ShapeDtypeStruct((rows, cols), bf16)
    ends = jnp.stack([strip > 0, strip < strips - 1, sub > 0]).astype(f32)

    def rows_at(block):
        return pl.ds(pl.multiple_of(block * deep, deep), deep)

    lane = 128
    chunk = 512 if cols % 512 == 0 else cols

    def inner(at):
        return pl.ds(lane + at, chunk)

    def laplace(source, block, at):
        wide = source[rows_at(block + 1), pl.ds(at, chunk + 2 * lane)]
        here = wide[:, lane : lane + chunk]
        row = lax.broadcasted_iota(jnp.int32, here.shape, 0)
        above = jnp.where(row == deep - 1, source[rows_at(block), inner(at)], here)
        below = jnp.where(row == 0, source[rows_at(block + 2), inner(at)], here)
        left = pltpu.roll(wide, 1, 1)[:, lane : lane + chunk]
        right = pltpu.roll(wide, chunk + 2 * lane - 1, 1)[:, lane : lane + chunk]
        return (
            pltpu.roll(above, 1, 0) + pltpu.roll(below, deep - 1, 0) + left + right - 4.0 * here
        )

    together = max(n for n in (1, 2, 3) if blocks % n == 0)

    def each_block(body):
        def several(trip, carry):
            for i in range(together):
                for at in range(0, cols, chunk):
                    body(trip * together + i, at)
            return carry

        lax.fori_loop(0, blocks // together, several, 0)

    def kept(ends_ref, block):
        return jnp.where(block == 0, ends_ref[0], jnp.where(block == blocks - 1, ends_ref[1], 1.0))

    padded = pltpu.VMEM((tall_rows + 2 * deep, cols + 2 * lane), f32)
    inside = pl.ds(deep, tall_rows), pl.ds(lane, cols)

    def clear_rims(*buffers):
        high, broad = tall_rows + 2 * deep, cols + 2 * lane
        for buffer in buffers:
            buffer[:deep, :] = jnp.zeros((deep, broad), f32)
            buffer[high - deep :, :] = jnp.zeros((deep, broad), f32)
            buffer[:, :lane] = jnp.zeros((high, lane), f32)
            buffer[:, broad - lane :] = jnp.zeros((high, lane), f32)

    def adjoint_body(ends_ref, mult, above, below, coef, pulled, middle, one, two, first, second):
        clear_rims(one, two)
        first[:deep, :] = above[...].astype(f32)
        first[deep : rows + deep, :] = mult[...]
        first[rows + deep :, :] = below[...].astype(f32)
        one[inside] = coef[...] * first[...]
        for step in range(STEPS):
            source, target = (one, two) if step % 2 == 0 else (two, one)
            now, later = (first, second) if step % 2 == 0 else (second, first)
            later = pulled if step == STEPS - 1 else later

            def advance(block, at):
                spot = rows_at(block), pl.ds(at, chunk)
                value = (now[spot] + laplace(source, block, at)) * kept(ends_ref, block)
                later[spot] = value
                if step < STEPS - 1:
                    target[rows_at(block + 1), inner(at)] = coef[spot] * value

            each_block(advance)
        middle[...] = pulled[deep : rows + deep, :].astype(bf16)

    def adjoint(multiplier, above, below):
        return pl.pallas_call(
            adjoint_body,
            out_shape=[wide_f32, field_bf16],
            in_specs=[scalars] + [whole] * 4,
            out_specs=[whole] * 2,
            scratch_shapes=[padded, padded] + [pltpu.VMEM((tall_rows, cols), f32)] * 2,
            compiler_params=limits,
            name="adjoint",
        )(ends, multiplier, above, below, diffuse_wide)

    def propagate(ends_ref, coef, one, two):
        for step in range(STEPS):
            source, target = (one, two) if step % 2 == 0 else (two, one)

            def advance(block, at):
                mid = rows_at(block + 1), inner(at)
                target[mid] = (
                    source[mid]
                    + coef[rows_at(block), pl.ds(at, chunk)] * laplace(source, block, at)
                ) * kept(ends_ref, block)

            each_block(advance)
        final = one if STEPS % 2 == 0 else two
        return final[2 * deep : rows + 2 * deep, lane : lane + cols]

    def begin_body(ends_ref, incr, own_coef, before, after, moved, one, two, coef):
        clear_rims(one, two)
        coef[:deep, :] = before[:deep, :].astype(f32)
        coef[deep : rows + deep, :] = own_coef[...]
        coef[rows + deep :, :] = after[:deep, :].astype(f32)
        one[deep : 2 * deep, lane : lane + cols] = before[deep:, :].astype(f32)
        one[2 * deep : rows + 2 * deep, lane : lane + cols] = incr[...]
        one[rows + 2 * deep : rows + 3 * deep, lane : lane + cols] = after[deep:, :].astype(f32)
        moved[...] = propagate(ends_ref, coef, one, two).astype(bf16)

    def begin(incr, before, after):
        return pl.pallas_call(
            begin_body,
            out_shape=field_bf16,
            in_specs=[scalars] + [whole] * 4,
            out_specs=whole,
            scratch_shapes=[padded, padded, pltpu.VMEM((tall_rows, cols), f32)],
            compiler_params=limits,
            name="begin",
        )(ends, incr, diffuse, before, after)

    def update_body(
        ends_ref, coef, past, arrived, pulled, mult, following, incr, forcing_ref,
        past_new, incr_new, target, grad, one, two
    ):
        clear_rims(one, two)
        past_new[...] = past[...] + step_weight * (
            arrived[...].astype(f32) - ends_ref[2] * pulled[...]
        )
        one[inside] = past_new[...]
        slope = mult[...] - following[...].astype(f32)
        grad[...] = slope
        incr_new[...] = incr[...] + step_weight * slope
        target[...] = forcing_ref[...] - incr_new[...] + propagate(ends_ref, coef, one, two)

    def update(past, arrived, pulled, mult, following, incr):
        return pl.pallas_call(
            update_body,
            out_shape=[wide_f32, field_f32, field_f32, field_f32],
            in_specs=[scalars] + [whole] * 8,
            out_specs=[whole] * 4,
            scratch_shapes=[padded, padded],
            compiler_params=limits,
            name="update",
        )(ends, diffuse_wide, past, arrived, pulled, mult, following, incr, forcing)

    short = jnp.concatenate(
        [diffuse.astype(jnp.bfloat16), incr_start[0].astype(jnp.bfloat16)], axis=0
    )
    lowest = jnp.concatenate([short[rows - deep : rows], short[2 * rows - deep :]], axis=0)
    topmost = jnp.concatenate([short[:deep], short[rows : rows + deep]], axis=0)
    before = to_strip(lowest, 1)
    after = to_strip(topmost, -1)
    moved = begin(incr_start[0], before, after)
    arrived = to_sub(moved, 1).astype(f32)
    far = to_sub(short, 1).astype(f32)
    far_rims = to_sub(jnp.concatenate([before, after], axis=0), 1).astype(f32)
    diffuse_wide = jnp.concatenate(
        [far_rims[:deep], far[:rows], far_rims[2 * deep : 3 * deep]], axis=0
    )
    past_wide = jnp.concatenate(
        [far_rims[deep : 2 * deep], far[rows:], far_rims[3 * deep :]], axis=0
    )

    def advance(target, multiplier, incr, past_wide, tile):
        multiplier = multiplier + step_weight * (target - finish(tile))
        low = multiplier.astype(bf16)
        pieces = cut(low)
        above = to_strip(low[rows - deep :], 1)
        below = to_strip(low[:deep], -1)
        pulled, middle = adjoint(multiplier, above, below)
        following = to_sub(middle, -1)
        arrived = to_sub(jnp.concatenate([above, low, below], axis=0), 1)
        tile = product(spread(pieces))
        past_wide, incr, target, grad = update(
            past_wide, arrived, pulled, multiplier, following, incr
        )
        return target, multiplier, incr, past_wide, tile, grad

    multiplier = mult_start[0]
    incr = incr_start[0]
    tile = product(spread(cut(multiplier.astype(jnp.bfloat16))))
    target = forcing - incr + arrived
    for _ in range(ITERS):
        target, multiplier, incr, past_wide, tile, grad = advance(
            target, multiplier, incr, past_wide, tile
        )
    mult_resid = target - finish(tile)
    return (mult_resid[None], grad[None])


def solution(mesh):
    return jax.shard_map(
        whole_step,
        mesh=mesh,
        in_specs=(
            P("sub", "strip", None),
            P("sub", "strip", None),
            P("sub", "strip", None),
            P("sub", "strip", None),
            P("strip", None),
            P(),
        ),
        out_specs=(P("sub", "strip", None), P("sub", "strip", None)),
        check_vma=False,
    )
```

```python
import jax
import jax.numpy as jnp
from jax import lax
from jax.experimental import pallas as pl
from jax.experimental.pallas import tpu as pltpu
from jax.sharding import PartitionSpec as P


STEPS = 4
ITERS = 2

step_weight = 0.5
BOTH = ("sub", "strip")


def split_strip(size):
    core = 2 if size % 2 == 0 else 1
    chips = size // core
    outer = 4 if chips % 4 == 0 else 1
    return outer, chips // outer, core


def whole_step(forcing, mult_start, incr_start, diffusivity, north_corr, east_corr):
    forcing = forcing[0]
    diffuse = diffusivity[0]
    rows, cols = forcing.shape
    strips = lax.axis_size("strip")
    subs = lax.axis_size("sub")
    nz, ny, nk = split_strip(strips)
    width = cols // nz
    strip = lax.axis_index("strip")
    sub = lax.axis_index("sub")
    my_z, my_y, my_k = strip // (ny * nk), (strip // nk) % ny, strip % nk

    def send(value, move):
        pairs = []
        for s in range(subs):
            for t in range(strips):
                to = move(s, t)
                if to is not None:
                    pairs.append((s * strips + t, to[0] * strips + to[1]))
        return lax.ppermute(value, BOTH, pairs)

    def by_z(value, j):
        return send(value, lambda s, t: (s, t ^ (j * ny * nk)))

    def by_y(value, j):
        return send(value, lambda s, t: (s, t ^ (j * nk)))

    def by_k(value, j):
        return send(value, lambda s, t: (s, t ^ j))

    def to_strip(value, step):
        return send(value, lambda s, t: (s, t + step) if 0 <= t + step < strips else None)

    def to_sub(value, step):
        return send(value, lambda s, t: (s + step, t) if 0 <= s + step < subs else None)

    def xor_order(value, axis, index):
        size = value.shape[axis]
        bit = 1
        while bit < size:
            order = [i ^ bit for i in range(size)]
            flipped = jnp.concatenate(
                [lax.slice_in_dim(value, i, i + 1, axis=axis) for i in order], axis=axis
            )
            value = jnp.where((index // bit) % 2 == 1, flipped, value)
            bit *= 2
        return value

    share = 2 if subs % 2 == 0 and rows % 32 == 0 else 1
    half = rows // share
    first = (sub % share) * half
    gathered = {0: lax.dynamic_slice_in_dim(north_corr, first, half, axis=0)}
    bit = nz // 2
    while bit >= 1:
        for j, part in list(gathered.items()):
            gathered[j ^ bit] = by_z(part, bit)
        bit //= 2
    north_rel = lax.dynamic_update_slice(
        jnp.zeros((nz * rows, strips * rows), jnp.bfloat16), north_corr, (0, 0)
    )
    for j in range(1, nz):
        north_rel = lax.dynamic_update_slice(north_rel, gathered[j], (j * rows + first, 0))
        if share == 2:
            other = send(gathered[j], lambda s, t: (s ^ 1, t))
            north_rel = lax.dynamic_update_slice(north_rel, other, (j * rows + half - first, 0))

    def cut(low):
        return [lax.dynamic_slice_in_dim(low, (my_z ^ j) * width, width, axis=1) for j in range(nz)]

    def spread(own):
        side = 2 if nz % 2 == 0 else 1
        held = {0: own[0]}
        for j in [*range(side, nz), *range(1, side)]:
            held[j] = by_z(own[j], j)
        groups = {
            (0, 0, at // side): xor_order(
                jnp.stack([held[j] for j in range(at, at + side)]), 0, my_z % side
            )
            for at in range(0, nz, side)
        }
        for jy in range(1, ny):
            for i in range(nz // side):
                groups[0, jy, i] = by_y(groups[0, 0, i], jy)
        for jk in range(1, nk):
            for jy in range(ny):
                for i in range(nz // side):
                    groups[jk, jy, i] = by_k(groups[0, jy, i], jk)
        tall = jnp.zeros((nz, ny * nk, rows, width), jnp.bfloat16)
        for (jk, jy, i), group in groups.items():
            at = ((my_z // side) ^ i) * side, (my_y ^ jy) * nk + (my_k ^ jk), 0, 0
            tall = lax.dynamic_update_slice(tall, group[:, None], at)
        return tall.reshape(strips * rows, width)

    def product(tall):
        tile = jnp.dot(north_rel, tall, preferred_element_type=jnp.float32).astype(jnp.bfloat16)
        return [tile[j * rows : (j + 1) * rows] for j in range(nz)]

    def finish(tile):
        parts = [tile[0]] + [by_z(tile[j], j) for j in range(1, nz)]
        line = xor_order(jnp.stack(parts), 0, my_z).transpose(1, 0, 2).reshape(rows, cols)
        return jnp.dot(line, east_corr, preferred_element_type=jnp.float32)

    deep = 8
    tall_rows = rows + 2 * deep
    blocks = tall_rows // deep
    whole = pl.BlockSpec(memory_space=pltpu.VMEM)
    scalars = pl.BlockSpec(memory_space=pltpu.SMEM)
    limits = pltpu.CompilerParams(vmem_limit_bytes=20 * 1024 * 1024)
    f32, bf16 = jnp.float32, jnp.bfloat16
    wide_f32 = jax.ShapeDtypeStruct((tall_rows, cols), f32)
    field_f32 = jax.ShapeDtypeStruct((rows, cols), f32)
    field_bf16 = jax.ShapeDtypeStruct((rows, cols), bf16)
    ends = jnp.stack([strip > 0, strip < strips - 1, sub > 0]).astype(f32)

    def rows_at(block):
        return pl.ds(pl.multiple_of(block * deep, deep), deep)

    lane = 128
    chunk = 512 if cols % 512 == 0 else cols

    def inner(at):
        return pl.ds(lane + at, chunk)

    def laplace(source, block, at):
        wide = source[rows_at(block + 1), pl.ds(at, chunk + 2 * lane)]
        here = wide[:, lane : lane + chunk]
        row = lax.broadcasted_iota(jnp.int32, here.shape, 0)
        above = jnp.where(row == deep - 1, source[rows_at(block), inner(at)], here)
        below = jnp.where(row == 0, source[rows_at(block + 2), inner(at)], here)
        left = pltpu.roll(wide, 1, 1)[:, lane : lane + chunk]
        right = pltpu.roll(wide, chunk + 2 * lane - 1, 1)[:, lane : lane + chunk]
        return (
            pltpu.roll(above, 1, 0) + pltpu.roll(below, deep - 1, 0) + left + right - 4.0 * here
        )

    together = max(n for n in (1, 2, 3, 6) if blocks % n == 0)

    def each_block(body):
        def several(trip, carry):
            for i in range(together):
                for at in range(0, cols, chunk):
                    body(trip * together + i, at)
            return carry

        lax.fori_loop(0, blocks // together, several, 0)

    def kept(ends_ref, block):
        return jnp.where(block == 0, ends_ref[0], jnp.where(block == blocks - 1, ends_ref[1], 1.0))

    padded = pltpu.VMEM((tall_rows + 2 * deep, cols + 2 * lane), f32)
    inside = pl.ds(deep, tall_rows), pl.ds(lane, cols)

    def clear_rims(*buffers):
        high, broad = tall_rows + 2 * deep, cols + 2 * lane
        for buffer in buffers:
            buffer[:deep, :] = jnp.zeros((deep, broad), f32)
            buffer[high - deep :, :] = jnp.zeros((deep, broad), f32)
            buffer[:, :lane] = jnp.zeros((high, lane), f32)
            buffer[:, broad - lane :] = jnp.zeros((high, lane), f32)

    def adjoint_body(ends_ref, mult, above, below, coef, pulled, middle, one, two, first, second):
        clear_rims(one, two)
        first[:deep, :] = above[...].astype(f32)
        first[deep : rows + deep, :] = mult[...]
        first[rows + deep :, :] = below[...].astype(f32)
        one[inside] = coef[...] * first[...]
        for step in range(STEPS):
            source, target = (one, two) if step % 2 == 0 else (two, one)
            now, later = (first, second) if step % 2 == 0 else (second, first)
            later = pulled if step == STEPS - 1 else later

            def advance(block, at):
                spot = rows_at(block), pl.ds(at, chunk)
                value = (now[spot] + laplace(source, block, at)) * kept(ends_ref, block)
                later[spot] = value
                if step < STEPS - 1:
                    target[rows_at(block + 1), inner(at)] = coef[spot] * value

            each_block(advance)
        middle[...] = pulled[deep : rows + deep, :].astype(bf16)

    def adjoint(multiplier, above, below):
        return pl.pallas_call(
            adjoint_body,
            out_shape=[wide_f32, field_bf16],
            in_specs=[scalars] + [whole] * 4,
            out_specs=[whole] * 2,
            scratch_shapes=[padded, padded] + [pltpu.VMEM((tall_rows, cols), f32)] * 2,
            compiler_params=limits,
            name="adjoint",
        )(ends, multiplier, above, below, diffuse_wide)

    def propagate(ends_ref, coef, one, two):
        for step in range(STEPS):
            source, target = (one, two) if step % 2 == 0 else (two, one)

            def advance(block, at):
                mid = rows_at(block + 1), inner(at)
                target[mid] = (
                    source[mid]
                    + coef[rows_at(block), pl.ds(at, chunk)] * laplace(source, block, at)
                ) * kept(ends_ref, block)

            each_block(advance)
        final = one if STEPS % 2 == 0 else two
        return final[2 * deep : rows + 2 * deep, lane : lane + cols]

    def begin_body(ends_ref, incr, own_coef, before, after, moved, one, two, coef):
        clear_rims(one, two)
        coef[:deep, :] = before[:deep, :].astype(f32)
        coef[deep : rows + deep, :] = own_coef[...]
        coef[rows + deep :, :] = after[:deep, :].astype(f32)
        one[deep : 2 * deep, lane : lane + cols] = before[deep:, :].astype(f32)
        one[2 * deep : rows + 2 * deep, lane : lane + cols] = incr[...]
        one[rows + 2 * deep : rows + 3 * deep, lane : lane + cols] = after[deep:, :].astype(f32)
        moved[...] = propagate(ends_ref, coef, one, two).astype(bf16)

    def begin(incr, before, after):
        return pl.pallas_call(
            begin_body,
            out_shape=field_bf16,
            in_specs=[scalars] + [whole] * 4,
            out_specs=whole,
            scratch_shapes=[padded, padded, pltpu.VMEM((tall_rows, cols), f32)],
            compiler_params=limits,
            name="begin",
        )(ends, incr, diffuse, before, after)

    def update_body(ends_ref, coef, past, arrived, pulled, past_new, moved, one, two):
        clear_rims(one, two)
        past_new[...] = past[...] + step_weight * (
            arrived[...].astype(f32) - ends_ref[2] * pulled[...]
        )
        one[inside] = past_new[...]
        moved[...] = propagate(ends_ref, coef, one, two)

    def update(past, arrived, pulled):
        return pl.pallas_call(
            update_body,
            out_shape=[wide_f32, field_f32],
            in_specs=[scalars] + [whole] * 4,
            out_specs=[whole] * 2,
            scratch_shapes=[padded, padded],
            compiler_params=limits,
            name="update",
        )(ends, diffuse_wide, past, arrived, pulled)

    short = jnp.concatenate(
        [diffuse.astype(jnp.bfloat16), incr_start[0].astype(jnp.bfloat16)], axis=0
    )
    lowest = jnp.concatenate([short[rows - deep : rows], short[2 * rows - deep :]], axis=0)
    topmost = jnp.concatenate([short[:deep], short[rows : rows + deep]], axis=0)
    before = to_strip(lowest, 1)
    after = to_strip(topmost, -1)
    moved = begin(incr_start[0], before, after)
    arrived = to_sub(moved, 1).astype(f32)
    far = to_sub(short, 1).astype(f32)
    far_rims = to_sub(jnp.concatenate([before, after], axis=0), 1).astype(f32)
    diffuse_wide = jnp.concatenate(
        [far_rims[:deep], far[:rows], far_rims[2 * deep : 3 * deep]], axis=0
    )
    past_wide = jnp.concatenate(
        [far_rims[deep : 2 * deep], far[rows:], far_rims[3 * deep :]], axis=0
    )

    def advance(target, multiplier, incr, past_wide, tile):
        multiplier = multiplier + step_weight * (target - finish(tile))
        low = multiplier.astype(bf16)
        pieces = cut(low)
        above = to_strip(low[rows - deep :], 1)
        below = to_strip(low[:deep], -1)
        pulled, middle = adjoint(multiplier, above, below)
        following = to_sub(middle, -1)
        arrived = to_sub(jnp.concatenate([above, low, below], axis=0), 1)
        tile = product(spread(pieces))
        past_wide, moved = update(past_wide, arrived, pulled)
        grad = multiplier - following.astype(f32)
        incr = incr + step_weight * grad
        target = forcing - incr + moved
        return target, multiplier, incr, past_wide, tile, grad

    multiplier = mult_start[0]
    incr = incr_start[0]
    tile = product(spread(cut(multiplier.astype(jnp.bfloat16))))
    target = forcing - incr + arrived
    for _ in range(ITERS):
        target, multiplier, incr, past_wide, tile, grad = advance(
            target, multiplier, incr, past_wide, tile
        )
    target, grad = lax.optimization_barrier((target, grad))
    mult_resid = target - finish(tile)
    return (mult_resid[None], grad[None])


def solution(mesh):
    return jax.shard_map(
        whole_step,
        mesh=mesh,
        in_specs=(
            P("sub", "strip", None),
            P("sub", "strip", None),
            P("sub", "strip", None),
            P("sub", "strip", None),
            P("strip", None),
            P(),
        ),
        out_specs=(P("sub", "strip", None), P("sub", "strip", None)),
        check_vma=False,
    )
```
